32 devices in a mesh: dp: 16 (over z, y, core), vocab: 2 (over x).
Axes of the slice: x: 2, y: 2, z: 4, core: 2. Of those that a mesh axis runs over, the one named last changes fastest.
Arguments:
- hidden: bfloat16 [2048, 3072], P(('dp', 'vocab')), may hold values from -128 to 128
- targets: int32 [2048], P(('dp', 'vocab')), may hold values from 0 to 4095
- lengths: int32 [16], P('dp'), may hold values from 1 to 128
- head: bfloat16 [3072, 4096], P('dp', 'vocab'), may hold values from -1 to 1
Outputs:
- grad_hidden: bfloat16 [2048, 3072], P(('dp', 'vocab'))
- loss: float32 [], replicated
The draws below stay inside these ranges and needn't reach their ends.
All inputs are finite; a program needn't handle non-finite values.
Results may differ from the reference program's by a relative error of at most 0.0052.
Values may be sent and summed in bfloat16 or wider, within the bound.
No kernel may reach another device: no remote copies, remote signals or barrier semaphores. Data moves between devices by JAX's collectives and lax.ppermute only.
A program may use at most 64 MiB of HBM per device.

```python
import jax
import jax.numpy as jnp
from jax import lax

D = 3072
CLIP = 128
LEVELS = 4096
TOKENS = 2048
N_DP = 16


def head_values(key):
    base_key = jax.random.fold_in(key, 11)
    values = jax.random.normal(base_key, (D, LEVELS), jnp.float32) * (3.0 / D ** 0.5)
    return jnp.clip(values, -1.0, 1.0)


def draw_head(key, part):
    return head_values(key).astype(jnp.bfloat16)


def draw_hidden(key, part):
    values = jnp.clip(jax.random.normal(jax.random.fold_in(key, 23), (TOKENS, D), jnp.float32), -6.0, 6.0)
    return values.astype(jnp.bfloat16)


def plant(result, stream_key, smallest, high):
    longest = result.shape.index(max(result.shape))
    spots = []
    for shift in (0, 1):
        where = [jax.random.randint(jax.random.fold_in(stream_key, axis), (), 0, length) for axis, length in enumerate(result.shape)]
        where[longest] = (where[longest] + shift) % result.shape[longest]
        spots.append(tuple(where))
    return result.at[spots[0]].set(smallest).at[spots[1]].set(high)


def setup_inputs(seed: int = 0) -> dict:
    splits = jax.random.split(jax.random.key(seed), 5)
    return {
        "hidden": draw_hidden(jax.random.fold_in(splits[4], 71), 0),
        "targets": plant(jax.random.randint(splits[1], (TOKENS,), 0, LEVELS), jax.random.fold_in(splits[1], 1), 0, LEVELS - 1).astype(jnp.int32),
        "lengths": plant(jax.random.randint(splits[2], (N_DP,), 1, CLIP + 1), jax.random.fold_in(splits[2], 1), 1, CLIP).astype(jnp.int32),
        "head": draw_head(jax.random.fold_in(splits[4], 71), 0),
    }


def clip_terms(clip_rows, clip_targets, clip_length, head, total_count):
    logits = jnp.dot(clip_rows, head, preferred_element_type=jnp.float32)
    maxima = jnp.max(logits, axis=1)
    totals = jnp.sum(jnp.exp(logits - maxima[:, None]), axis=1)
    log_total = maxima + jnp.log(totals)
    level_grid = jnp.arange(head.shape[1], dtype=jnp.int32)
    is_target = clip_targets[:, None] == level_grid[None, :]
    target_logit = jnp.sum(jnp.where(is_target, logits, 0.0), axis=1)
    positions = jnp.arange(clip_rows.shape[0], dtype=jnp.int32)
    valid_rows = (positions < clip_length).astype(jnp.float32)
    loss_sum = jnp.sum(valid_rows * (log_total - target_logit))
    weights = (valid_rows / total_count)[:, None]
    grad_logits = (weights * (jnp.exp(logits - log_total[:, None]) - is_target.astype(jnp.float32))).astype(jnp.bfloat16)
    grad_rows = lax.dot_general(grad_logits, head, (((1,), (1,)), ((), ())), preferred_element_type=jnp.float32)
    return grad_rows.astype(jnp.bfloat16), loss_sum


def reference(hidden, targets, lengths, head):
    total_count = jnp.sum(lengths).astype(jnp.float32)

    def one_clip(clip_items):
        return clip_terms(clip_items[0], clip_items[1], clip_items[2], head, total_count)

    grad_blocks, loss_sums = lax.map(one_clip, (hidden.reshape(N_DP, CLIP, D), targets.reshape(N_DP, CLIP), lengths))
    return grad_blocks.reshape(TOKENS, D), jnp.sum(loss_sums) / total_count
```

```python
import jax
import jax.numpy as jnp
from jax import lax
from jax.sharding import PartitionSpec as P


def swap(value, dp_bits, vocab_bits, dp_size, vocab_size):
    pairs = [
        (d * vocab_size + v, (d ^ dp_bits) * vocab_size + (v ^ vocab_bits))
        for d in range(dp_size)
        for v in range(vocab_size)
    ]
    return lax.ppermute(value, ("dp", "vocab"), pairs)


def build(dp_size, vocab_size):
    CORE, SIDE, PAIR = 1, 2, 4
    assert dp_size >= 8 and dp_size & (dp_size - 1) == 0
    assert vocab_size & (vocab_size - 1) == 0
    far_steps = range(2 * PAIR, dp_size, 2 * PAIR)

    def dp_swap(value, bits):
        return swap(value, bits, 0, dp_size, vocab_size)

    def vocab_swap(value, bits):
        return swap(value, 0, bits, dp_size, vocab_size)

    def over_vocab(piece):
        return [piece] + [vocab_swap(piece, bits) for bits in range(1, vocab_size)]

    def gather_vocab_first(piece):
        near = over_vocab(piece)
        side = dp_swap(jnp.stack(near), SIDE)
        return near, [side[i] for i in range(vocab_size)]

    def gather_side_first(piece):
        both = jnp.stack([piece, dp_swap(piece, SIDE)])
        spread = over_vocab(both)
        return [s[0] for s in spread], [s[1] for s in spread]

    def local(hidden, targets, lengths, head):
        dp = lax.axis_index("dp")
        vocab = lax.axis_index("vocab")
        core = dp & 1
        parity = (dp >> 2) & 1
        home_rows = hidden.shape[0]
        feature_rows = head.shape[0]
        shard_levels = head.shape[1]
        width = shard_levels // 4
        splits = 2 if vocab_size == 2 else 1
        half = width // splits

        def level_class(par, cor):
            return lax.dynamic_slice_in_dim(head, (par * 2 + cor) * width, width, 1)

        def ordered(mine, other):
            return jnp.where(core == 0, jnp.concatenate([mine, other]), jnp.concatenate([other, mine]))

        out_own = level_class(parity, 1 - core)
        out_pair = level_class(1 - parity, 1 - core)
        in_own = dp_swap(out_own, CORE)
        in_pair = dp_swap(out_pair, CORE)
        own = ordered(level_class(parity, core), in_own)
        for_pair = ordered(level_class(1 - parity, core), in_pair)
        pair = dp_swap(for_pair, PAIR)

        pieces = {}

        def split(piece):
            return [piece[:, k * half : (k + 1) * half] for k in range(splits)]

        def spread_split(base, piece):
            if splits == 1:
                return spread(base, piece, True)
            a, b = split(piece)
            a0, a1 = gather_vocab_first(a)
            b0, b1 = gather_side_first(b)
            pieces[base] = [[x, y] for x, y in zip(a0, b0)]
            pieces[base | 1] = [[x, y] for x, y in zip(a1, b1)]

        def spread(base, piece, vocab_first):
            p0, p1 = (gather_vocab_first if vocab_first else gather_side_first)(piece)
            pieces[base] = [split(x) for x in p0]
            pieces[base | 1] = [split(x) for x in p1]

        spread_split(0, own)
        far_own = {bits: dp_swap(own, bits) for bits in far_steps}
        far_pair = {bits: dp_swap(pair, bits) for bits in far_steps}
        spread(PAIR >> 1, pair, True)
        for bits in far_steps:
            spread(bits >> 1, far_own[bits], False)
            spread_split((bits | PAIR) >> 1, far_pair[bits])
        blocks = sorted(pieces)

        hidden_pair = dp_swap(hidden, PAIR)
        hidden_core = dp_swap(jnp.stack([hidden, hidden_pair]), CORE)
        rows = jnp.concatenate([hidden, hidden_core[0], hidden_pair, hidden_core[1]])
        facts = jnp.concatenate([targets, lengths])[None]
        facts_pair = jnp.concatenate([facts, dp_swap(facts, PAIR)])
        facts_core = dp_swap(facts_pair, CORE)
        facts = jnp.stack([facts_pair[0], facts_core[0], facts_pair[1], facts_core[1]])
        group_targets = facts[:, :home_rows].reshape(-1)
        group_lengths = facts[:, home_rows]
        total_count = jnp.sum(group_lengths)
        for bits in [SIDE, *(1 << k for k in range(3, dp_size.bit_length() - 1))]:
            total_count = total_count + dp_swap(jnp.full((1, 128), total_count), bits)[0, 0]
        total_count = total_count.astype(jnp.float32)
        positions = vocab * home_rows + jnp.arange(home_rows, dtype=jnp.int32)
        valid = (positions[None] < group_lengths[:, None]).astype(jnp.float32).reshape(-1)

        span = 2 * feature_rows
        chip = dp >> 1
        parts = [
            lax.dynamic_slice_in_dim(rows, (block ^ chip) * span, span, 1) for block in blocks
        ]
        tiles = [(offset, k) for offset in range(vocab_size) for k in range(splits)]
        logits = []
        for offset, k in tiles:
            total = None
            for block in blocks:
                term = jnp.dot(
                    parts[block], pieces[block][offset][k], preferred_element_type=jnp.float32
                )
                total = term if total is None else total + term
            logits.append(total)
        is_target = []
        for offset, k in tiles:
            base = (vocab ^ offset) * shard_levels + (parity * 2 + core) * width + k * half
            grid = base + jnp.arange(half, dtype=jnp.int32)
            is_target.append(group_targets[:, None] == grid[None])
        maxima = jnp.max(jnp.stack([jnp.max(t, axis=1) for t in logits]), axis=0)
        totals = sum(jnp.sum(jnp.exp(t - maxima[:, None]), axis=1) for t in logits)
        target_logit = sum(
            jnp.sum(jnp.where(hit, t, 0.0), axis=1) for hit, t in zip(is_target, logits)
        )
        stats = jnp.stack([maxima, totals, target_logit]).reshape(3, 2, 2, home_rows)
        for bits, axis in ((CORE, 2), (PAIR, 1)):
            other = jnp.flip(dp_swap(stats, bits), axis)
            top = jnp.maximum(stats[0], other[0])
            total = stats[1] * jnp.exp(stats[0] - top) + other[1] * jnp.exp(other[0] - top)
            stats = jnp.stack([top, total, stats[2] + other[2]])
        stats = stats.reshape(3, -1)
        log_total = stats[0] + jnp.log(stats[1])

        loss = jnp.sum((valid * (log_total - stats[2]))[:home_rows])
        loss = jnp.full((1, 128), loss)
        for k in range(dp_size.bit_length() - 1):
            loss = loss + dp_swap(loss, 1 << k)
        for k in range(vocab_size.bit_length() - 1):
            loss = loss + vocab_swap(loss, 1 << k)
        loss = loss[0, 0] / total_count

        weights = (valid / total_count)[:, None]
        grads = [
            (weights * (jnp.exp(t - log_total[:, None]) - hit.astype(jnp.float32))).astype(jnp.bfloat16)
            for hit, t in zip(is_target, logits)
        ]
        columns = []
        for block in blocks:
            total = None
            for g, (offset, k) in zip(grads, tiles):
                term = lax.dot_general(
                    g,
                    pieces[block][offset][k],
                    (((1,), (1,)), ((), ())),
                    preferred_element_type=jnp.float32,
                )
                total = term if total is None else total + term
            columns.append(total.reshape(2, 2, home_rows, span))
        partial = jnp.stack(columns)
        other = dp_swap(partial[:, :, 1].astype(jnp.bfloat16), CORE)
        partial = partial[:, :, 0] + other.astype(jnp.float32)
        away = partial[:, 1].astype(jnp.bfloat16)
        flipped = jnp.stack([away[block ^ (PAIR >> 1)] for block in blocks])
        other = dp_swap(flipped, PAIR)
        final = (partial[:, 0] + other.astype(jnp.float32)).astype(jnp.bfloat16)
        order = jnp.arange(len(blocks)) ^ chip
        final = final[order].transpose(1, 0, 2).reshape(home_rows, -1)
        return final, loss

    return local


def solution(mesh):
    placed = (P(("dp", "vocab"), None), P(("dp", "vocab")), P("dp"), P("dp", "vocab"))
    return jax.shard_map(
        build(mesh.shape["dp"], mesh.shape["vocab"]),
        mesh=mesh,
        in_specs=placed,
        out_specs=(P(("dp", "vocab"), None), P()),
        check_vma=False,
    )
```

```python
import functools

import jax
import jax.numpy as jnp
from jax import lax
from jax.experimental import pallas as pl
from jax.experimental.pallas import tpu as pltpu
from jax.sharding import PartitionSpec as P


CORE, SIDE, PAIR = 1, 2, 4
LANES = 128
VMEM = pl.BlockSpec(memory_space=pltpu.VMEM)
SMEM = pl.BlockSpec(memory_space=pltpu.SMEM)


def accumulate(plan, pieces, rows_ref, logits_ref):
    for block, start, size, number, lead in plan:
        piece = pieces[number][...] if lead is None else pieces[number][lead]
        logits_ref[:, start : start + size] += jnp.dot(
            rows_ref[block], piece, preferred_element_type=jnp.float32
        )


def early_kernel(plan, rows_ref, *refs):
    *pieces, logits_ref = refs
    logits_ref[...] = jnp.zeros_like(logits_ref)
    accumulate(plan, pieces, rows_ref, logits_ref)


def stats_kernel(plan, width, place_ref, rows_ref, facts_ref, early_ref, *refs):
    *pieces, logits_ref, stats_ref = refs
    count, total_width = logits_ref.shape
    logits_ref[...] = early_ref[...]
    accumulate(plan, pieces, rows_ref, logits_ref)
    target = facts_ref[:, :1]
    maxima = jnp.max(logits_ref[...], axis=1, keepdims=True)
    totals = jnp.zeros_like(maxima)
    hit_logit = jnp.zeros_like(maxima)
    lane = lax.broadcasted_iota(jnp.int32, (count, width), 1)
    for offset in range(total_width // width):
        tile = logits_ref[:, offset * width : (offset + 1) * width]
        totals += jnp.sum(jnp.exp(tile - maxima), axis=1, keepdims=True)
        hit = lane == target - place_ref[3 + offset]
        hit_logit += jnp.sum(jnp.where(hit, tile, 0.0), axis=1, keepdims=True)
    column = lax.broadcasted_iota(jnp.int32, (count, LANES), 1)
    packed = jnp.where(column == 0, maxima, jnp.where(column == 1, totals, hit_logit))
    stats_ref[...] = jnp.transpose(packed)[:8]


def by_place(values, low, high):
    a, b, c, d = values
    a, b, c, d = (
        jnp.where(low, b, a),
        jnp.where(low, a, b),
        jnp.where(low, d, c),
        jnp.where(low, c, d),
    )
    return (
        jnp.where(high, c, a),
        jnp.where(high, d, b),
        jnp.where(high, a, c),
        jnp.where(high, b, d),
    )


def grad_kernel(plan, width, blocks, place_ref, count_ref, facts_ref, logits_ref, *refs):
    stats_refs, refs = refs[:4], refs[4:]
    *pieces, send_ref, keep_ref, loss_ref, grad_ref = refs
    count, total_width = logits_ref.shape
    home = count // 4
    low, high = place_ref[0] == 1, place_ref[1] == 1
    columns = jnp.transpose(
        jnp.concatenate(
            [ref[...] for ref in stats_refs] + [jnp.zeros((LANES - 32, count), jnp.float32)]
        )
    )
    members = []
    for k in range(4):
        column = columns[:, 8 * k : 8 * k + 8]
        members.append(
            jnp.concatenate([column[(r ^ k) * home : ((r ^ k) + 1) * home] for r in range(4)])
        )
    top = functools.reduce(jnp.maximum, [m[:, 0:1] for m in members])
    terms = by_place([m[:, 1:2] * jnp.exp(m[:, 0:1] - top) for m in members], low, high)
    log_total = top + jnp.log((terms[0] + terms[1]) + (terms[2] + terms[3]))
    hits = by_place([m[:, 2:3] for m in members], low, high)
    hit_logit = (hits[0] + hits[1]) + (hits[2] + hits[3])
    position = place_ref[2] + lax.rem(lax.broadcasted_iota(jnp.int32, (count, 1), 0), home)
    valid = (position < facts_ref[:, LANES - 1 :]).astype(jnp.float32)
    row_loss = valid * (log_total - hit_logit)
    sums = [
        jnp.sum(row_loss[r * home : (r + 1) * home], axis=0, keepdims=True) for r in range(4)
    ]
    sums = by_place(sums, low, high)
    loss_ref[...] = jnp.broadcast_to((sums[0] + sums[1]) + (sums[2] + sums[3]), loss_ref.shape)
    weight = valid / count_ref[:1, :1].astype(jnp.float32)
    target = facts_ref[:, :1]
    lane = lax.broadcasted_iota(jnp.int32, (count, width), 1)
    for offset in range(total_width // width):
        tile = slice(offset * width, (offset + 1) * width)
        hit = (lane == target - place_ref[3 + offset]).astype(jnp.float32)
        grad_ref[:, tile] = (weight * (jnp.exp(logits_ref[:, tile] - log_total) - hit)).astype(
            jnp.bfloat16
        )
    for block in range(blocks):
        total = None
        for owner, start, size, number, lead in plan:
            if owner != block:
                continue
            piece = pieces[number][...] if lead is None else pieces[number][lead]
            term = lax.dot_general(
                grad_ref[:, start : start + size],
                piece,
                (((1,), (1,)), ((), ())),
                preferred_element_type=jnp.float32,
            )
            total = term if total is None else total + term
        keep_ref[block, :home] = total[:home]
        send_ref[block, :home] = total[home : 2 * home].astype(jnp.bfloat16)
        keep_ref[block, home:] = total[2 * home : 3 * home]
        send_ref[block, home:] = total[3 * home :].astype(jnp.bfloat16)


def build(dp_size, vocab_size):
    assert dp_size >= 8 and dp_size & (dp_size - 1) == 0
    assert vocab_size & (vocab_size - 1) == 0
    far_steps = range(2 * PAIR, dp_size, 2 * PAIR)
    far_bits = [1 << k for k in range(3, dp_size.bit_length() - 1)]
    blocks = dp_size // 2

    def swap(value, dp_bits, vocab_bits=0):
        pairs = [
            (d * vocab_size + v, (d ^ dp_bits) * vocab_size + (v ^ vocab_bits))
            for d in range(dp_size)
            for v in range(vocab_size)
        ]
        return lax.ppermute(value, ("dp", "vocab"), pairs)

    def local(hidden, targets, lengths, head):
        dp = lax.axis_index("dp")
        vocab = lax.axis_index("vocab")
        core = dp & 1
        parity = (dp >> 2) & 1
        chip = dp >> 1
        home = hidden.shape[0]
        features = head.shape[0]
        shard_levels = head.shape[1]
        width = shard_levels // 4
        splits = 2 if vocab_size == 2 else 1
        half = width // splits
        span = 2 * features

        def level_class(par, cor):
            return lax.dynamic_slice_in_dim(head, (par * 2 + cor) * width, width, 1)

        def ordered(mine, other):
            return jnp.where(
                core == 0, jnp.concatenate([mine, other]), jnp.concatenate([other, mine])
            )

        def over_vocab(piece):
            return [swap(piece, 0, bits) for bits in range(1, vocab_size)]

        arrays, plan = [], []

        def use(array, *places):
            for block, start, size, lead in places:
                plan.append((block, start, size, len(arrays), lead))
            arrays.append(array)

        def vocab_first(base, piece, start, size):
            near = over_vocab(piece)
            for i, x in enumerate(near):
                use(x, (base, (i + 1) * width + start, size, None))
            side = swap(jnp.stack([piece, *near]), SIDE)
            use(side, *[(base | 1, o * width + start, size, o) for o in range(vocab_size)])

        def side_first(base, piece, start, size):
            side = swap(piece, SIDE)
            use(side, (base | 1, start, size, None))
            for i, x in enumerate(over_vocab(jnp.stack([piece, side]))):
                at = (i + 1) * width + start
                use(x, (base, at, size, 0), (base | 1, at, size, 1))

        def spread(base, piece, mode):
            use(piece, (base, 0, width, None))
            if mode == "both" and splits == 2:
                vocab_first(base, piece[:, :half], 0, half)
                side_first(base, piece[:, half:], half, half)
            elif mode == "side":
                side_first(base, piece, 0, width)
            else:
                vocab_first(base, piece, 0, width)

        own_other = swap(level_class(parity, 1 - core), CORE)
        own = ordered(level_class(parity, core), own_other)
        pair_other = swap(level_class(1 - parity, 1 - core), CORE)
        for_pair = ordered(level_class(1 - parity, core), pair_other)
        far_own = {bits: swap(own, bits) for bits in far_steps}
        pair = swap(for_pair, PAIR)
        far_pair = {bits: swap(pair, bits) for bits in far_steps}
        spread(0, own, "both")
        spread(PAIR >> 1, pair, "vocab")
        for bits in far_steps:
            spread(bits >> 1, far_own[bits], "side")
        late = len(arrays)
        for bits in far_steps:
            spread((bits | PAIR) >> 1, far_pair[bits], "both")

        facts = jnp.where(
            jnp.arange(LANES)[None] == LANES - 1, lengths[:, None], targets[:, None]
        )
        facts_pair = swap(facts, PAIR)
        facts_core = swap(jnp.stack([facts, facts_pair]), CORE)
        facts = jnp.concatenate([facts, facts_core[0], facts_pair, facts_core[1]])
        hidden_pair = swap(hidden, PAIR)
        hidden_core = swap(jnp.stack([hidden, hidden_pair]), CORE)
        rows = jnp.concatenate([hidden, hidden_core[0], hidden_pair, hidden_core[1]])
        rows = jnp.stack(
            [lax.dynamic_slice_in_dim(rows, (b ^ chip) * span, span, 1) for b in range(blocks)]
        )
        count = jnp.broadcast_to(
            jnp.sum(facts.reshape(4, home, LANES)[:, :1, LANES - 1 :], axis=0), (8, LANES)
        )
        for bits in [SIDE, *far_bits]:
            count = count + swap(count, bits)
        place = jnp.stack(
            [core, parity, vocab * home]
            + [
                (vocab ^ o) * shard_levels + (parity * 2 + core) * width for o in range(vocab_size)
            ]
        )

        count_rows, columns = 4 * home, vocab_size * width
        early_plan = [p for p in plan if p[3] < late]
        late_plan = [(b, s, z, n - late, l) for b, s, z, n, l in plan if n >= late]

        def cost(work, arrays, extra):
            moved = sum(a.size * a.dtype.itemsize for a in arrays)
            flops = sum(2 * count_rows * span * p[2] for p in work)
            return pl.CostEstimate(flops=flops, bytes_accessed=moved, transcendentals=extra)

        logits_shape = jax.ShapeDtypeStruct((count_rows, columns), jnp.float32)
        early = pl.pallas_call(
            functools.partial(early_kernel, early_plan),
            out_shape=logits_shape,
            in_specs=[VMEM] * (1 + late),
            out_specs=VMEM,
            cost_estimate=cost(early_plan, [rows, *arrays[:late]], 0),
            name="early_logits",
        )(rows, *arrays[:late])
        logits, stats = pl.pallas_call(
            functools.partial(stats_kernel, late_plan, width),
            out_shape=(logits_shape, jax.ShapeDtypeStruct((8, count_rows), jnp.float32)),
            in_specs=[SMEM] + [VMEM] * (3 + len(arrays) - late),
            out_specs=(VMEM, VMEM),
            cost_estimate=cost(late_plan, [rows, *arrays[late:]], count_rows * columns),
            name="row_stats",
        )(place, rows, facts, early, *arrays[late:])
        others = [swap(stats, CORE), swap(stats, PAIR), swap(stats, CORE | PAIR)]
        send, keep, loss = pl.pallas_call(
            functools.partial(grad_kernel, plan, width, blocks),
            out_shape=(
                jax.ShapeDtypeStruct((blocks, 2 * home, span), jnp.bfloat16),
                jax.ShapeDtypeStruct((blocks, 2 * home, span), jnp.float32),
                jax.ShapeDtypeStruct((8, LANES), jnp.float32),
            ),
            in_specs=[SMEM] + [VMEM] * (7 + len(arrays)),
            out_specs=(VMEM, VMEM, VMEM),
            scratch_shapes=[pltpu.VMEM((count_rows, columns), jnp.bfloat16)],
            cost_estimate=cost(plan, arrays, count_rows * columns),
            name="grad_rows",
        )(place, count, facts, logits, stats, *others, *arrays)

        other = swap(send, CORE)
        total = keep + other.astype(jnp.float32)
        away = swap(total[:, home:].astype(jnp.bfloat16), PAIR)
        for k in range(vocab_size.bit_length() - 1):
            loss = loss + swap(loss, 0, 1 << k)
        for bits in [SIDE, *far_bits]:
            loss = loss + swap(loss, bits)
        loss = loss[0, 0] / count[0, 0].astype(jnp.float32)
        order = jnp.arange(blocks) ^ chip
        final = total[:, :home][order] + away[order ^ (PAIR >> 1)].astype(jnp.float32)
        final = final.astype(jnp.bfloat16).transpose(1, 0, 2).reshape(home, -1)
        return final, loss

    return local


def solution(mesh):
    placed = (P(("dp", "vocab"), None), P(("dp", "vocab")), P("dp"), P("dp", "vocab"))
    sizes = mesh.shape["dp"], mesh.shape["vocab"]
    return jax.shard_map(
        build(*sizes),
        mesh=mesh,
        in_specs=placed,
        out_specs=(P(("dp", "vocab"), None), P()),
        check_vma=False,
    )
```

```python
import functools

import jax
import jax.numpy as jnp
from jax import lax
from jax.experimental import pallas as pl
from jax.experimental.pallas import tpu as pltpu
from jax.sharding import PartitionSpec as P


CORE, SIDE, PAIR = 1, 2, 4
LANES = 128
VMEM = pl.BlockSpec(memory_space=pltpu.VMEM)
SMEM = pl.BlockSpec(memory_space=pltpu.SMEM)


def accumulate(plan, pieces, rows_ref, logits_ref):
    for block, start, size, number, lead in plan:
        piece = pieces[number][...] if lead is None else pieces[number][lead]
        logits_ref[:, start : start + size] += jnp.dot(
            rows_ref[block], piece, preferred_element_type=jnp.float32
        )


def early_kernel(plan, rows_ref, *refs):
    *pieces, logits_ref = refs
    logits_ref[...] = jnp.zeros_like(logits_ref)
    accumulate(plan, pieces, rows_ref, logits_ref)


def stats_kernel(plan, width, place_ref, rows_ref, facts_ref, early_ref, *refs):
    *pieces, logits_ref, stats_ref = refs
    count, total_width = logits_ref.shape
    logits_ref[...] = early_ref[...]
    accumulate(plan, pieces, rows_ref, logits_ref)
    target = facts_ref[:, :1]
    maxima = jnp.max(logits_ref[...], axis=1, keepdims=True)
    totals = jnp.zeros_like(maxima)
    hit_logit = jnp.zeros_like(maxima)
    lane = lax.broadcasted_iota(jnp.int32, (count, width), 1)
    for offset in range(total_width // width):
        tile = logits_ref[:, offset * width : (offset + 1) * width]
        totals += jnp.sum(jnp.exp(tile - maxima), axis=1, keepdims=True)
        hit = lane == target - place_ref[3 + offset]
        hit_logit += jnp.sum(jnp.where(hit, tile, 0.0), axis=1, keepdims=True)
    column = lax.broadcasted_iota(jnp.int32, (count, LANES), 1)
    packed = jnp.where(column == 0, maxima, jnp.where(column == 1, totals, hit_logit))
    stats_ref[...] = jnp.transpose(packed)[:8]


def by_place(values, low, high):
    a, b, c, d = values
    a, b, c, d = (
        jnp.where(low, b, a),
        jnp.where(low, a, b),
        jnp.where(low, d, c),
        jnp.where(low, c, d),
    )
    return (
        jnp.where(high, c, a),
        jnp.where(high, d, b),
        jnp.where(high, a, c),
        jnp.where(high, b, d),
    )


def grad_kernel(plan, width, chunk, place_ref, count_ref, facts_ref, logits_ref, *refs):
    stats_refs, refs = refs[:4], refs[4:]
    *pieces, send_ref, keep_ref, loss_ref, grad_ref = refs
    count, total_width = logits_ref.shape
    home = count // 4
    low, high = place_ref[0] == 1, place_ref[1] == 1
    columns = jnp.transpose(
        jnp.concatenate(
            [ref[...] for ref in stats_refs] + [jnp.zeros((LANES - 32, count), jnp.float32)]
        )
    )
    members = []
    for k in range(4):
        column = columns[:, 8 * k : 8 * k + 8]
        members.append(
            jnp.concatenate([column[(r ^ k) * home : ((r ^ k) + 1) * home] for r in range(4)])
        )
    top = functools.reduce(jnp.maximum, [m[:, 0:1] for m in members])
    terms = by_place([m[:, 1:2] * jnp.exp(m[:, 0:1] - top) for m in members], low, high)
    log_total = top + jnp.log((terms[0] + terms[1]) + (terms[2] + terms[3]))
    hits = by_place([m[:, 2:3] for m in members], low, high)
    hit_logit = (hits[0] + hits[1]) + (hits[2] + hits[3])
    position = place_ref[2] + lax.rem(lax.broadcasted_iota(jnp.int32, (count, 1), 0), home)
    valid = (position < facts_ref[:, LANES - 1 :]).astype(jnp.float32)
    row_loss = valid * (log_total - hit_logit)
    sums = [
        jnp.sum(row_loss[r * home : (r + 1) * home], axis=0, keepdims=True) for r in range(4)
    ]
    sums = by_place(sums, low, high)
    loss_ref[...] = jnp.broadcast_to((sums[0] + sums[1]) + (sums[2] + sums[3]), loss_ref.shape)
    weight = valid / count_ref[:1, :1].astype(jnp.float32)
    target = facts_ref[:, :1]
    lane = lax.broadcasted_iota(jnp.int32, (count, width), 1)
    for offset in range(total_width // width):
        tile = slice(offset * width, (offset + 1) * width)
        hit = (lane == target - place_ref[3 + offset]).astype(jnp.float32)
        grad_ref[:, tile] = (weight * (jnp.exp(logits_ref[:, tile] - log_total) - hit)).astype(
            jnp.bfloat16
        )
    grad_product(plan, chunk, pieces, grad_ref, send_ref, keep_ref)


def grad_product(plan, chunk, pieces, grad_ref, send_ref, keep_ref):
    home = grad_ref.shape[0] // 4
    for row, block in enumerate(chunk):
        total = None
        for owner, start, size, number, lead in plan:
            if owner != block:
                continue
            piece = pieces[number][...] if lead is None else pieces[number][lead]
            term = lax.dot_general(
                grad_ref[:, start : start + size],
                piece,
                (((1,), (1,)), ((), ())),
                preferred_element_type=jnp.float32,
            )
            total = term if total is None else total + term
        keep_ref[row, :home] = total[:home]
        send_ref[row, :home] = total[home : 2 * home].astype(jnp.bfloat16)
        keep_ref[row, home:] = total[2 * home : 3 * home]
        send_ref[row, home:] = total[3 * home :].astype(jnp.bfloat16)


def rest_kernel(plan, chunk, grad_ref, *refs):
    *pieces, send_ref, keep_ref = refs
    grad_product(plan, chunk, pieces, grad_ref, send_ref, keep_ref)


def build(dp_size, vocab_size):
    assert dp_size >= 8 and dp_size & (dp_size - 1) == 0
    assert vocab_size & (vocab_size - 1) == 0
    far_steps = range(2 * PAIR, dp_size, 2 * PAIR)
    far_bits = [1 << k for k in range(3, dp_size.bit_length() - 1)]
    blocks = dp_size // 2

    def swap(value, dp_bits, vocab_bits=0):
        pairs = [
            (d * vocab_size + v, (d ^ dp_bits) * vocab_size + (v ^ vocab_bits))
            for d in range(dp_size)
            for v in range(vocab_size)
        ]
        return lax.ppermute(value, ("dp", "vocab"), pairs)

    def local(hidden, targets, lengths, head):
        dp = lax.axis_index("dp")
        vocab = lax.axis_index("vocab")
        core = dp & 1
        parity = (dp >> 2) & 1
        chip = dp >> 1
        home = hidden.shape[0]
        features = head.shape[0]
        shard_levels = head.shape[1]
        width = shard_levels // 4
        splits = 2 if vocab_size == 2 else 1
        half = width // splits
        span = 2 * features

        def level_class(par, cor):
            return lax.dynamic_slice_in_dim(head, (par * 2 + cor) * width, width, 1)

        def ordered(mine, other):
            return jnp.where(
                core == 0, jnp.concatenate([mine, other]), jnp.concatenate([other, mine])
            )

        def over_vocab(piece):
            return [swap(piece, 0, bits) for bits in range(1, vocab_size)]

        arrays, plan = [], []

        def use(array, *places):
            for block, start, size, lead in places:
                plan.append((block, start, size, len(arrays), lead))
            arrays.append(array)

        def vocab_first(base, piece, start, size):
            near = over_vocab(piece)
            for i, x in enumerate(near):
                use(x, (base, (i + 1) * width + start, size, None))
            side = swap(jnp.stack([piece, *near]), SIDE)
            use(side, *[(base | 1, o * width + start, size, o) for o in range(vocab_size)])

        def side_first(base, piece, start, size):
            side = swap(piece, SIDE)
            use(side, (base | 1, start, size, None))
            for i, x in enumerate(over_vocab(jnp.stack([piece, side]))):
                at = (i + 1) * width + start
                use(x, (base, at, size, 0), (base | 1, at, size, 1))

        def spread(base, piece, mode):
            use(piece, (base, 0, width, None))
            if mode == "both" and splits == 2:
                vocab_first(base, piece[:, :half], 0, half)
                side_first(base, piece[:, half:], half, half)
            elif mode == "side":
                side_first(base, piece, 0, width)
            else:
                vocab_first(base, piece, 0, width)

        pair_other = swap(level_class(1 - parity, 1 - core), CORE)
        own_other = swap(level_class(parity, 1 - core), CORE)
        own = ordered(level_class(parity, core), own_other)
        for_pair = ordered(level_class(1 - parity, core), pair_other)
        far_own = {bits: swap(own, bits) for bits in far_steps}
        pair = swap(for_pair, PAIR)
        far_pair = {bits: swap(for_pair, bits | PAIR) for bits in far_steps}
        spread(0, own, "both")
        spread(PAIR >> 1, pair, "both")
        for bits in far_steps:
            spread(bits >> 1, far_own[bits], "both")
        late = len(arrays)
        for bits in far_steps:
            spread((bits | PAIR) >> 1, far_pair[bits], "both")

        facts = jnp.where(
            jnp.arange(LANES)[None] == LANES - 1, lengths[:, None], targets[:, None]
        )
        facts_pair = swap(facts, PAIR)
        facts_core = swap(jnp.stack([facts, facts_pair]), CORE)
        facts = jnp.concatenate([facts, facts_core[0], facts_pair, facts_core[1]])
        hidden_pair = swap(hidden, PAIR)
        hidden_core = swap(jnp.stack([hidden, hidden_pair]), CORE)
        rows = jnp.concatenate([hidden, hidden_core[0], hidden_pair, hidden_core[1]])
        rows = jnp.stack(
            [lax.dynamic_slice_in_dim(rows, (b ^ chip) * span, span, 1) for b in range(blocks)]
        )
        count = jnp.broadcast_to(
            jnp.sum(facts.reshape(4, home, LANES)[:, :1, LANES - 1 :], axis=0), (8, LANES)
        )
        for bits in [SIDE, *far_bits]:
            count = count + swap(count, bits)
        place = jnp.stack(
            [core, parity, vocab * home]
            + [
                (vocab ^ o) * shard_levels + (parity * 2 + core) * width for o in range(vocab_size)
            ]
        )

        count_rows, columns = 4 * home, vocab_size * width
        early_plan = [p for p in plan if p[3] < late]
        late_plan = [(b, s, z, n - late, l) for b, s, z, n, l in plan if n >= late]

        def cost(work, arrays, extra):
            moved = sum(a.size * a.dtype.itemsize for a in arrays)
            flops = sum(2 * count_rows * span * p[2] for p in work)
            return pl.CostEstimate(flops=flops, bytes_accessed=moved, transcendentals=extra)

        def limit(arrays, extra_mib):
            size = sum(a.size * a.dtype.itemsize for a in arrays) + 10 * count_rows * columns
            return pltpu.CompilerParams(vmem_limit_bytes=size + (extra_mib << 20))

        logits_shape = jax.ShapeDtypeStruct((count_rows, columns), jnp.float32)
        early = pl.pallas_call(
            functools.partial(early_kernel, early_plan),
            out_shape=logits_shape,
            in_specs=[VMEM] * (1 + late),
            out_specs=VMEM,
            cost_estimate=cost(early_plan, [rows, *arrays[:late]], 0),
            compiler_params=limit([rows, *arrays[:late]], 4),
            name="early_logits",
        )(rows, *arrays[:late])
        logits, stats = pl.pallas_call(
            functools.partial(stats_kernel, late_plan, width),
            out_shape=(logits_shape, jax.ShapeDtypeStruct((8, count_rows), jnp.float32)),
            in_specs=[SMEM] + [VMEM] * (3 + len(arrays) - late),
            out_specs=(VMEM, VMEM),
            cost_estimate=cost(late_plan, [rows, *arrays[late:]], count_rows * columns),
            compiler_params=limit([rows, *arrays[late:]], 4),
            name="row_stats",
        )(place, rows, facts, early, *arrays[late:])
        others = [swap(stats, CORE), swap(stats, PAIR), swap(stats, CORE | PAIR)]
        chunks = [range(0, blocks // 2), range(blocks // 2, blocks)]

        def part(chunk):
            chosen = [p for p in plan if p[0] in chunk]
            numbers = sorted({p[3] for p in chosen})
            at = {n: i for i, n in enumerate(numbers)}
            return [(b, s, z, at[n], l) for b, s, z, n, l in chosen], [arrays[n] for n in numbers]

        def halves_shape(chunk):
            shape = (len(chunk), 2 * home, span)
            return (
                jax.ShapeDtypeStruct(shape, jnp.bfloat16),
                jax.ShapeDtypeStruct(shape, jnp.float32),
            )

        grad_plan, grad_arrays = part(chunks[0])
        send, keep, loss, grad = pl.pallas_call(
            functools.partial(grad_kernel, grad_plan, width, chunks[0]),
            out_shape=(
                *halves_shape(chunks[0]),
                jax.ShapeDtypeStruct((8, LANES), jnp.float32),
                jax.ShapeDtypeStruct((count_rows, columns), jnp.bfloat16),
            ),
            in_specs=[SMEM] + [VMEM] * (7 + len(grad_arrays)),
            out_specs=(VMEM,) * 4,
            cost_estimate=cost(grad_plan, grad_arrays, count_rows * columns),
            compiler_params=limit(grad_arrays, 8),
            name="grad_rows",
        )(place, count, facts, logits, stats, *others, *grad_arrays)
        rest_plan, rest_arrays = part(chunks[1])
        send_rest, keep_rest = pl.pallas_call(
            functools.partial(rest_kernel, rest_plan, chunks[1]),
            out_shape=halves_shape(chunks[1]),
            in_specs=[VMEM] * (1 + len(rest_arrays)),
            out_specs=(VMEM,) * 2,
            cost_estimate=cost(rest_plan, rest_arrays, 0),
            compiler_params=limit(rest_arrays, 4),
            name="grad_rest",
        )(grad, *rest_arrays)

        totals, aways = [], []
        for s, k in ((send, keep), (send_rest, keep_rest)):
            total = k + swap(s, CORE).astype(jnp.float32)
            totals.append(total[:, :home])
            aways.append(swap(total[:, home:].astype(jnp.bfloat16), PAIR))
        total, away = jnp.concatenate(totals), jnp.concatenate(aways)
        for k in range(vocab_size.bit_length() - 1):
            loss = loss + swap(loss, 0, 1 << k)
        for bits in [SIDE, *far_bits]:
            loss = loss + swap(loss, bits)
        loss = loss[0, 0] / count[0, 0].astype(jnp.float32)
        order = jnp.arange(blocks) ^ chip
        final = total[order] + away[order ^ (PAIR >> 1)].astype(jnp.float32)
        final = final.astype(jnp.bfloat16).transpose(1, 0, 2).reshape(home, -1)
        return final, loss

    return local


def solution(mesh):
    placed = (P(("dp", "vocab"), None), P(("dp", "vocab")), P("dp"), P("dp", "vocab"))
    sizes = mesh.shape["dp"], mesh.shape["vocab"]
    return jax.shard_map(
        build(*sizes),
        mesh=mesh,
        in_specs=placed,
        out_specs=(P(("dp", "vocab"), None), P()),
        check_vma=False,
    )
```

```python
import functools

import jax
import jax.numpy as jnp
from jax import lax
from jax.experimental import pallas as pl
from jax.experimental.pallas import tpu as pltpu
from jax.sharding import PartitionSpec as P


CORE, SIDE, PAIR = 1, 2, 4
LANES = 128
VMEM = pl.BlockSpec(memory_space=pltpu.VMEM)
SMEM = pl.BlockSpec(memory_space=pltpu.SMEM)


def accumulate(plan, pieces, rows_ref, logits_ref):
    for block, start, size, number, lead in plan:
        piece = pieces[number][...] if lead is None else pieces[number][lead]
        logits_ref[:, start : start + size] += jnp.dot(
            rows_ref[block], piece, preferred_element_type=jnp.float32
        )


def early_kernel(plan, rows_ref, *refs):
    *pieces, logits_ref = refs
    logits_ref[...] = jnp.zeros_like(logits_ref)
    accumulate(plan, pieces, rows_ref, logits_ref)


def stats_kernel(plan, width, place_ref, rows_ref, facts_ref, early_ref, *refs):
    *pieces, logits_ref, stats_ref = refs
    count, total_width = logits_ref.shape
    logits_ref[...] = early_ref[...]
    accumulate(plan, pieces, rows_ref, logits_ref)
    target = facts_ref[:, :1]
    maxima = jnp.max(logits_ref[...], axis=1, keepdims=True)
    totals = jnp.zeros_like(maxima)
    hit_logit = jnp.zeros_like(maxima)
    lane = lax.broadcasted_iota(jnp.int32, (count, width), 1)
    for offset in range(total_width // width):
        tile = logits_ref[:, offset * width : (offset + 1) * width]
        totals += jnp.sum(jnp.exp(tile - maxima), axis=1, keepdims=True)
        hit = lane == target - place_ref[3 + offset]
        hit_logit += jnp.sum(jnp.where(hit, tile, 0.0), axis=1, keepdims=True)
    column = lax.broadcasted_iota(jnp.int32, (count, LANES), 1)
    packed = jnp.where(column == 0, maxima, jnp.where(column == 1, totals, hit_logit))
    stats_ref[...] = jnp.transpose(packed)[:8]


def by_place(values, low, high):
    a, b, c, d = values
    a, b, c, d = (
        jnp.where(low, b, a),
        jnp.where(low, a, b),
        jnp.where(low, d, c),
        jnp.where(low, c, d),
    )
    return (
        jnp.where(high, c, a),
        jnp.where(high, d, b),
        jnp.where(high, a, c),
        jnp.where(high, b, d),
    )


def grad_kernel(plan, width, chunk, place_ref, count_ref, facts_ref, logits_ref, *refs):
    stats_refs, refs = refs[:4], refs[4:]
    *pieces, send_ref, keep_ref, loss_ref, grad_ref = refs
    count, total_width = logits_ref.shape
    home = count // 4
    low, high = place_ref[0] == 1, place_ref[1] == 1
    columns = jnp.transpose(
        jnp.concatenate(
            [ref[...] for ref in stats_refs] + [jnp.zeros((LANES - 32, count), jnp.float32)]
        )
    )
    members = []
    for k in range(4):
        column = columns[:, 8 * k : 8 * k + 8]
        members.append(
            jnp.concatenate([column[(r ^ k) * home : ((r ^ k) + 1) * home] for r in range(4)])
        )
    top = functools.reduce(jnp.maximum, [m[:, 0:1] for m in members])
    terms = by_place([m[:, 1:2] * jnp.exp(m[:, 0:1] - top) for m in members], low, high)
    log_total = top + jnp.log((terms[0] + terms[1]) + (terms[2] + terms[3]))
    hits = by_place([m[:, 2:3] for m in members], low, high)
    hit_logit = (hits[0] + hits[1]) + (hits[2] + hits[3])
    position = place_ref[2] + lax.rem(lax.broadcasted_iota(jnp.int32, (count, 1), 0), home)
    valid = (position < facts_ref[:, LANES - 1 :]).astype(jnp.float32)
    row_loss = valid * (log_total - hit_logit)
    sums = [
        jnp.sum(row_loss[r * home : (r + 1) * home], axis=0, keepdims=True) for r in range(4)
    ]
    sums = by_place(sums, low, high)
    loss_ref[...] = jnp.broadcast_to((sums[0] + sums[1]) + (sums[2] + sums[3]), loss_ref.shape)
    weight = valid / count_ref[:1, :1].astype(jnp.float32)
    target = facts_ref[:, :1]
    lane = lax.broadcasted_iota(jnp.int32, (count, width), 1)
    for offset in range(total_width // width):
        tile = slice(offset * width, (offset + 1) * width)
        hit = (lane == target - place_ref[3 + offset]).astype(jnp.float32)
        grad_ref[:, tile] = (weight * (jnp.exp(logits_ref[:, tile] - log_total) - hit)).astype(
            jnp.bfloat16
        )
    grad_product(plan, chunk, pieces, grad_ref, send_ref, keep_ref)


def grad_product(plan, chunk, pieces, grad_ref, send_ref, keep_ref):
    home = grad_ref.shape[0] // 4
    for row, block in enumerate(chunk):
        total = None
        for owner, start, size, number, lead in plan:
            if owner != block:
                continue
            piece = pieces[number][...] if lead is None else pieces[number][lead]
            term = lax.dot_general(
                grad_ref[:, start : start + size],
                piece,
                (((1,), (1,)), ((), ())),
                preferred_element_type=jnp.float32,
            )
            total = term if total is None else total + term
        keep_ref[row, :home] = total[:home]
        send_ref[row, :home] = total[home : 2 * home].astype(jnp.bfloat16)
        keep_ref[row, home:] = total[2 * home : 3 * home]
        send_ref[row, home:] = total[3 * home :].astype(jnp.bfloat16)


def rest_kernel(plan, chunk, grad_ref, *refs):
    *pieces, send_ref, keep_ref = refs
    grad_product(plan, chunk, pieces, grad_ref, send_ref, keep_ref)


def final_kernel(chunk, chip_ref, *refs):
    *parts, out_ref = refs
    totals, aways = parts[:2], parts[2:]
    home = out_ref.shape[0]
    span = totals[0].shape[2]
    first_half = chip_ref[0] < chunk
    turn = lax.rem(chip_ref[0], chunk)
    for half in range(2):
        for row in range(chunk):
            at = row ^ turn
            columns = slice((half * chunk + row) * span, (half * chunk + row + 1) * span)
            for own, other in ((0, first_half), (1, jnp.logical_not(first_half))):
                source = half ^ own

                @pl.when(other)
                def _():
                    value = totals[source][at, :home] + aways[source][at ^ (PAIR >> 1)].astype(
                        jnp.float32
                    )
                    out_ref[:, columns] = value.astype(jnp.bfloat16)


def build(dp_size, vocab_size):
    assert dp_size >= 8 and dp_size & (dp_size - 1) == 0
    assert vocab_size & (vocab_size - 1) == 0
    far_steps = range(2 * PAIR, dp_size, 2 * PAIR)
    far_bits = [1 << k for k in range(3, dp_size.bit_length() - 1)]
    blocks = dp_size // 2

    def swap(value, dp_bits, vocab_bits=0):
        pairs = [
            (d * vocab_size + v, (d ^ dp_bits) * vocab_size + (v ^ vocab_bits))
            for d in range(dp_size)
            for v in range(vocab_size)
        ]
        return lax.ppermute(value, ("dp", "vocab"), pairs)

    def local(hidden, targets, lengths, head):
        dp = lax.axis_index("dp")
        vocab = lax.axis_index("vocab")
        core = dp & 1
        parity = (dp >> 2) & 1
        chip = dp >> 1
        home = hidden.shape[0]
        features = head.shape[0]
        shard_levels = head.shape[1]
        width = shard_levels // 4
        splits = 2 if vocab_size == 2 else 1
        half = width // splits
        span = 2 * features

        def level_class(par, cor):
            return lax.dynamic_slice_in_dim(head, (par * 2 + cor) * width, width, 1)

        def ordered(mine, other):
            return jnp.where(
                core == 0, jnp.concatenate([mine, other]), jnp.concatenate([other, mine])
            )

        def over_vocab(piece):
            return [swap(piece, 0, bits) for bits in range(1, vocab_size)]

        arrays, plan = [], []

        def use(array, *places):
            for block, start, size, lead in places:
                plan.append((block, start, size, len(arrays), lead))
            arrays.append(array)

        def vocab_first(base, piece, start, size):
            near = over_vocab(piece)
            for i, x in enumerate(near):
                use(x, (base, (i + 1) * width + start, size, None))
            side = swap(jnp.stack([piece, *near]), SIDE)
            use(side, *[(base | 1, o * width + start, size, o) for o in range(vocab_size)])

        def side_first(base, piece, start, size):
            side = swap(piece, SIDE)
            use(side, (base | 1, start, size, None))
            for i, x in enumerate(over_vocab(jnp.stack([piece, side]))):
                at = (i + 1) * width + start
                use(x, (base, at, size, 0), (base | 1, at, size, 1))

        def spread(base, piece, mode):
            use(piece, (base, 0, width, None))
            if mode == "both" and splits == 2:
                vocab_first(base, piece[:, :half], 0, half)
                side_first(base, piece[:, half:], half, half)
            elif mode == "side":
                side_first(base, piece, 0, width)
            else:
                vocab_first(base, piece, 0, width)

        pair_other = swap(level_class(1 - parity, 1 - core), CORE)
        own_other = swap(level_class(parity, 1 - core), CORE)
        own = ordered(level_class(parity, core), own_other)
        for_pair = ordered(level_class(1 - parity, core), pair_other)
        far_own = {bits: swap(own, bits) for bits in far_steps}
        pair = swap(for_pair, PAIR)
        far_pair = {bits: swap(for_pair, bits | PAIR) for bits in far_steps}
        spread(0, own, "both")
        spread(PAIR >> 1, pair, "both")
        for bits in far_steps:
            spread(bits >> 1, far_own[bits], "both")
        late = len(arrays)
        for bits in far_steps:
            spread((bits | PAIR) >> 1, far_pair[bits], "both")

        facts = jnp.where(
            jnp.arange(LANES)[None] == LANES - 1, lengths[:, None], targets[:, None]
        )
        facts_pair = swap(facts, PAIR)
        facts_both = jnp.stack([facts, facts_pair])
        facts_core = swap(facts_both, CORE)
        facts = jnp.concatenate([facts, facts_core[0], facts_pair, facts_core[1]])
        hidden_pair = swap(hidden, PAIR)
        hidden_both = jnp.stack([hidden, hidden_pair])
        hidden_core = swap(hidden_both, CORE)
        rows = jnp.concatenate([hidden, hidden_core[0], hidden_pair, hidden_core[1]])
        rows = jnp.stack(
            [lax.dynamic_slice_in_dim(rows, (b ^ chip) * span, span, 1) for b in range(blocks)]
        )
        count = jnp.broadcast_to(
            jnp.sum(facts.reshape(4, home, LANES)[:, :1, LANES - 1 :], axis=0), (8, LANES)
        )
        for bits in [SIDE, *far_bits]:
            count = count + swap(count, bits)
        place = jnp.stack(
            [core, parity, vocab * home]
            + [
                (vocab ^ o) * shard_levels + (parity * 2 + core) * width for o in range(vocab_size)
            ]
        )

        count_rows, columns = 4 * home, vocab_size * width
        early_plan = [p for p in plan if p[3] < late]
        late_plan = [(b, s, z, n - late, l) for b, s, z, n, l in plan if n >= late]

        def cost(work, arrays, extra):
            moved = sum(a.size * a.dtype.itemsize for a in arrays)
            flops = sum(2 * count_rows * span * p[2] for p in work)
            return pl.CostEstimate(flops=flops, bytes_accessed=moved, transcendentals=extra)

        def limit(arrays, extra_mib):
            size = sum(a.size * a.dtype.itemsize for a in arrays) + 10 * count_rows * columns
            return pltpu.CompilerParams(vmem_limit_bytes=size + (extra_mib << 20))

        logits_shape = jax.ShapeDtypeStruct((count_rows, columns), jnp.float32)
        early = pl.pallas_call(
            functools.partial(early_kernel, early_plan),
            out_shape=logits_shape,
            in_specs=[VMEM] * (1 + late),
            out_specs=VMEM,
            cost_estimate=cost(early_plan, [rows, *arrays[:late]], 0),
            compiler_params=limit([rows, *arrays[:late]], 4),
            name="early_logits",
        )(rows, *arrays[:late])
        logits, stats = pl.pallas_call(
            functools.partial(stats_kernel, late_plan, width),
            out_shape=(logits_shape, jax.ShapeDtypeStruct((8, count_rows), jnp.float32)),
            in_specs=[SMEM] + [VMEM] * (3 + len(arrays) - late),
            out_specs=(VMEM, VMEM),
            cost_estimate=cost(late_plan, [rows, *arrays[late:]], count_rows * columns),
            compiler_params=limit([rows, *arrays[late:]], 4),
            name="row_stats",
        )(place, rows, facts, early, *arrays[late:])
        others = [swap(stats, CORE), swap(stats, PAIR), swap(stats, CORE | PAIR)]
        chunks = [range(0, blocks // 2), range(blocks // 2, blocks)]

        def part(chunk):
            chosen = [p for p in plan if p[0] in chunk]
            numbers = sorted({p[3] for p in chosen})
            at = {n: i for i, n in enumerate(numbers)}
            return [(b, s, z, at[n], l) for b, s, z, n, l in chosen], [arrays[n] for n in numbers]

        def halves_shape(chunk):
            shape = (len(chunk), 2 * home, span)
            return (
                jax.ShapeDtypeStruct(shape, jnp.bfloat16),
                jax.ShapeDtypeStruct(shape, jnp.float32),
            )

        grad_plan, grad_arrays = part(chunks[0])
        send, keep, loss, grad = pl.pallas_call(
            functools.partial(grad_kernel, grad_plan, width, chunks[0]),
            out_shape=(
                *halves_shape(chunks[0]),
                jax.ShapeDtypeStruct((8, LANES), jnp.float32),
                jax.ShapeDtypeStruct((count_rows, columns), jnp.bfloat16),
            ),
            in_specs=[SMEM] + [VMEM] * (7 + len(grad_arrays)),
            out_specs=(VMEM,) * 4,
            cost_estimate=cost(grad_plan, grad_arrays, count_rows * columns),
            compiler_params=limit(grad_arrays, 8),
            name="grad_rows",
        )(place, count, facts, logits, stats, *others, *grad_arrays)
        rest_plan, rest_arrays = part(chunks[1])
        send_rest, keep_rest = pl.pallas_call(
            functools.partial(rest_kernel, rest_plan, chunks[1]),
            out_shape=halves_shape(chunks[1]),
            in_specs=[VMEM] * (1 + len(rest_arrays)),
            out_specs=(VMEM,) * 2,
            cost_estimate=cost(rest_plan, rest_arrays, 0),
            compiler_params=limit(rest_arrays, 4),
            name="grad_rest",
        )(grad, *rest_arrays)

        totals, aways = [], []
        for s, k in ((send, keep), (send_rest, keep_rest)):
            total = k + swap(s, CORE).astype(jnp.float32)
            totals.append(total)
            aways.append(swap(total[:, home:].astype(jnp.bfloat16), PAIR))
        for bits in [*far_bits, SIDE]:
            loss = loss + swap(loss, bits)
        for k in range(vocab_size.bit_length() - 1):
            loss = loss + swap(loss, 0, 1 << k)
        loss = loss[0, 0] / count[0, 0].astype(jnp.float32)
        final = pl.pallas_call(
            functools.partial(final_kernel, len(chunks[0])),
            out_shape=jax.ShapeDtypeStruct((home, blocks * span), jnp.bfloat16),
            in_specs=[SMEM] + [VMEM] * 4,
            out_specs=VMEM,
            compiler_params=pltpu.CompilerParams(vmem_limit_bytes=16 << 20),
            name="final_rows",
        )(chip.reshape(1), *totals, *aways)
        return final, loss

    return local


def solution(mesh):
    placed = (P(("dp", "vocab"), None), P(("dp", "vocab")), P("dp"), P("dp", "vocab"))
    sizes = mesh.shape["dp"], mesh.shape["vocab"]
    return jax.shard_map(
        build(*sizes),
        mesh=mesh,
        in_specs=placed,
        out_specs=(P(("dp", "vocab"), None), P()),
        check_vma=False,
    )
```

```python
import functools

import jax
import jax.numpy as jnp
from jax import lax
from jax.experimental import pallas as pl
from jax.experimental.pallas import tpu as pltpu
from jax.sharding import PartitionSpec as P


CORE, SIDE, PAIR, FAR = 1, 2, 4, 8
GROUP = FAR
LANES = 128
BASE = 128
VMEM = pl.BlockSpec(memory_space=pltpu.VMEM)
SMEM = pl.BlockSpec(memory_space=pltpu.SMEM)


def accumulate(plan, pieces, rows_ref, logits_ref, pile_ref):
    held = sorted({block for block, _, _ in plan})
    for (block, start, size), piece in zip(plan, pieces, strict=True):
        value = piece[...]
        pile_ref[held.index(block), :, start : start + size] = value
        logits_ref[:, start : start + size] += jnp.dot(
            rows_ref[block], value, preferred_element_type=jnp.float32
        )


def rows_kernel(blocks, chip_ref, *refs):
    *members, rows_ref, facts_ref, count_ref = refs
    home = members[0].shape[0]
    span = rows_ref.shape[2]
    lane = lax.broadcasted_iota(jnp.int32, (home, LANES), 1)
    total = None
    for r, member in enumerate(members):
        at = slice(r * home, (r + 1) * home)
        for block in range(blocks):
            rows_ref[block ^ chip_ref[0], at, :] = member[:, block * span : (block + 1) * span]
        notes = member[:, blocks * span :].astype(jnp.float32)
        target = (notes[:, 0:1] * BASE + notes[:, 1:2]).astype(jnp.int32)
        length = (notes[:, 2:3] * BASE + notes[:, 3:4]).astype(jnp.int32)
        facts_ref[at, :] = jnp.where(lane == LANES - 1, length, target)
        total = length[:1] if total is None else total + length[:1]
    count_ref[...] = jnp.broadcast_to(total, count_ref.shape)


def early_kernel(plan, rows_ref, *refs):
    *pieces, logits_ref, pile_ref = refs
    logits_ref[...] = jnp.zeros_like(logits_ref)
    accumulate(plan, pieces, rows_ref, logits_ref, pile_ref)


def stats_kernel(plan, width, place_ref, rows_ref, facts_ref, early_ref, far_ref, *refs):
    *pieces, logits_ref, pile_ref, stats_ref = refs
    count, total_width = logits_ref.shape
    logits_ref[...] = early_ref[...]
    accumulate(plan, pieces, rows_ref, logits_ref, pile_ref)
    target = facts_ref[:, :1]
    maxima = jnp.max(logits_ref[...], axis=1, keepdims=True)
    totals = jnp.zeros_like(maxima)
    hit_logit = jnp.zeros_like(maxima)
    lane = lax.broadcasted_iota(jnp.int32, (count, width), 1)
    for offset in range(total_width // width):
        tile = logits_ref[:, offset * width : (offset + 1) * width]
        totals += jnp.sum(jnp.exp(tile - maxima), axis=1, keepdims=True)
        hit = lane == target - place_ref[2 + offset]
        hit_logit += jnp.sum(jnp.where(hit, tile, 0.0), axis=1, keepdims=True)
    column = lax.broadcasted_iota(jnp.int32, (count, LANES), 1)
    packed = jnp.where(column == 0, maxima, jnp.where(column == 1, totals, hit_logit))
    packed = jnp.where(column == 3, far_ref[:1, :1].astype(jnp.float32), packed)
    stats_ref[...] = jnp.transpose(packed)[:8]


def by_place(values, place):
    for bit in (CORE, SIDE, PAIR):
        odd = lax.rem(place // bit, 2) == 1
        values = [jnp.where(odd, values[i ^ bit], values[i]) for i in range(GROUP)]
    return values


def tree_sum(values):
    while len(values) > 1:
        values = [a + b for a, b in zip(values[::2], values[1::2])]
    return values[0]


def grad_kernel(where, width, chunk, place_ref, count_ref, facts_ref, logits_ref, *refs):
    stats_refs, refs = refs[:4], refs[4:]
    *piles, send_ref, keep_ref, loss_ref, grad_ref = refs
    count, total_width = logits_ref.shape
    home = count // GROUP
    place = place_ref[0]
    members = []
    for k in range(GROUP):
        stats = stats_refs[k // 2][8 * (k % 2) : 8 * (k % 2) + 8, :]
        members.append(
            jnp.concatenate([stats[:, (r ^ k) * home : ((r ^ k) + 1) * home] for r in range(GROUP)], axis=1)
        )
    top = functools.reduce(jnp.maximum, [m[0:1] for m in members])
    terms = by_place([m[1:2] * jnp.exp(m[0:1] - top) for m in members], place)
    log_row = top + jnp.log(tree_sum(terms))
    hit_row = tree_sum(by_place([m[2:3] for m in members], place))
    columns = jnp.transpose(
        jnp.concatenate([log_row, hit_row, jnp.zeros((LANES - 2, count), jnp.float32)])
    )
    log_total, hit_logit = columns[:, 0:1], columns[:, 1:2]
    position = place_ref[1] + lax.rem(lax.broadcasted_iota(jnp.int32, (count, 1), 0), home)
    valid = (position < facts_ref[:, LANES - 1 :]).astype(jnp.float32)
    row_loss = valid * (log_total - hit_logit)
    sums = [
        jnp.sum(row_loss[r * home : (r + 1) * home], axis=0, keepdims=True) for r in range(GROUP)
    ]
    valid_count = count_ref[:1, :1].astype(jnp.float32) + sum(m[3:4, :1] for m in members)
    loss_ref[...] = jnp.broadcast_to(tree_sum(by_place(sums, place)) / valid_count, loss_ref.shape)
    weight = valid / valid_count
    target = facts_ref[:, :1]
    lane = lax.broadcasted_iota(jnp.int32, (count, width), 1)
    for offset in range(total_width // width):
        tile = slice(offset * width, (offset + 1) * width)
        hit = (lane == target - place_ref[2 + offset]).astype(jnp.float32)
        grad_ref[:, tile] = (weight * (jnp.exp(logits_ref[:, tile] - log_total) - hit)).astype(
            jnp.bfloat16
        )
    grad_product(where, chunk, piles, grad_ref, send_ref, keep_ref)


def grad_product(where, chunk, piles, grad_ref, send_ref, keep_ref):
    home = grad_ref.shape[0] // GROUP
    for row, block in enumerate(chunk):
        pile, index = where[block]
        total = lax.dot_general(
            grad_ref[...],
            piles[pile][index],
            (((1,), (1,)), ((), ())),
            preferred_element_type=jnp.float32,
        )
        for j in range(GROUP // 2):
            at = slice(j * home, (j + 1) * home)
            keep_ref[row, at] = total[2 * j * home : (2 * j + 1) * home]
            send_ref[row, at] = total[(2 * j + 1) * home : (2 * j + 2) * home].astype(jnp.bfloat16)


def rest_kernel(where, chunk, grad_ref, *refs):
    *piles, send_ref, keep_ref = refs
    grad_product(where, chunk, piles, grad_ref, send_ref, keep_ref)


def fold_kernel(taken, kept, sent, home, total_ref, *refs):
    *others, keep_ref, send_ref = refs
    for row, (block, array, index) in enumerate(taken):
        for j in range(len(kept)):
            at = slice(j * home, (j + 1) * home)
            rows = slice(kept[j] * home, (kept[j] + 1) * home)
            keep_ref[row, at] = total_ref[block, rows] + others[array][index, rows].astype(jnp.float32)
            rows = slice(sent[j] * home, (sent[j] + 1) * home)
            value = total_ref[block, rows] + others[array][index, rows].astype(jnp.float32)
            send_ref[row, at] = value.astype(jnp.bfloat16)


def final_kernel(sums, terms, shares, chip_ref, *refs):
    *arrays, out_ref, loss_ref, order_ref = refs
    loss_ref[...] = tree_sum([share[:1, :1] for share in arrays[len(arrays) - shares :]])
    blocks, _, span = order_ref.shape
    for block in range(blocks):
        (a, i), (b, j) = sums[block], terms[block]
        value = arrays[a][i] + arrays[b][j].astype(jnp.float32)
        order_ref[block ^ chip_ref[0]] = value.astype(jnp.bfloat16)
    for block in range(blocks):
        out_ref[:, block * span : (block + 1) * span] = order_ref[block]


def build(dp_size, vocab_size):
    assert dp_size >= 2 * GROUP and dp_size & (dp_size - 1) == 0
    assert vocab_size & (vocab_size - 1) == 0
    far_steps = range(GROUP, dp_size, GROUP)
    blocks = dp_size // 2

    def swap(value, dp_bits, vocab_bits=0):
        pairs = [
            (d * vocab_size + v, (d ^ dp_bits) * vocab_size + (v ^ vocab_bits))
            for d in range(dp_size)
            for v in range(vocab_size)
        ]
        return lax.ppermute(value, ("dp", "vocab"), pairs)

    def local(hidden, targets, lengths, head):
        dp = lax.axis_index("dp")
        vocab = lax.axis_index("vocab")
        core, chip, place = dp & 1, dp >> 1, dp & (GROUP - 1)
        home = hidden.shape[0]
        features = head.shape[0]
        shard_levels = head.shape[1]
        width = shard_levels // GROUP
        span = 2 * features
        arrays, plan = [], []

        def use(array, block, offset):
            plan.append((block, offset * width, width))
            arrays.append(array)

        def spread(block, piece):
            use(piece, block, 0)
            for bits in range(1, vocab_size):
                use(swap(piece, 0, bits), block, bits)

        def level_class(r):
            return lax.dynamic_slice_in_dim(head, (place ^ r) * width, width, 1)

        kinds = (0, PAIR, SIDE, SIDE | PAIR)
        arrived = swap(jnp.stack([level_class(CORE ^ r) for r in kinds]), CORE)
        ours = {}
        for i, r in enumerate(kinds):
            mine, other = level_class(r), arrived[i]
            ours[r] = jnp.where(
                core == 0, jnp.concatenate([mine, other]), jnp.concatenate([other, mine])
            )
        side = {0: swap(ours[SIDE], SIDE), PAIR: swap(ours[SIDE | PAIR], SIDE)}
        waves = [(ours, 0), (side, 1)]
        got = {}
        for source, bit in waves:
            got[bit] = source[0]
            got[(PAIR >> 1) | bit] = swap(source[PAIR], PAIR)
            for bits in far_steps:
                got[(bits >> 1) | bit] = swap(source[0], bits)
                got[((bits | PAIR) >> 1) | bit] = swap(source[PAIR], bits | PAIR)
        order = [b for b in range(blocks) if b & (PAIR >> 1) == 0 or b < 4]
        order += [b for b in range(blocks) if b not in order]
        late = None
        for block in order:
            if late is None and block & (PAIR >> 1) and block >= 4:
                late = len(arrays)
            spread(block, got[block])

        digits = [targets // BASE, targets % BASE, lengths // BASE, lengths % BASE]
        lane = jnp.arange(LANES)[None]
        notes = functools.reduce(
            lambda rest, i: jnp.where(lane == i, digits[i][:, None], rest), range(4), 0
        )
        mine = jnp.concatenate([hidden, notes.astype(hidden.dtype)], axis=1)
        pair = swap(mine, PAIR)
        beside = swap(mine, SIDE)
        both = swap(pair, SIDE)
        members = []
        for value in (mine, beside, pair, both):
            members += [value, swap(value, CORE)]
        count_rows, columns = GROUP * home, vocab_size * width
        rows, facts, count = pl.pallas_call(
            functools.partial(rows_kernel, blocks),
            out_shape=(
                jax.ShapeDtypeStruct((blocks, count_rows, span), hidden.dtype),
                jax.ShapeDtypeStruct((count_rows, LANES), jnp.int32),
                jax.ShapeDtypeStruct((8, LANES), jnp.int32),
            ),
            in_specs=[SMEM] + [VMEM] * GROUP,
            out_specs=(VMEM,) * 3,
            cost_estimate=pl.CostEstimate(
                flops=0, bytes_accessed=4 * count_rows * hidden.shape[1], transcendentals=0
            ),
            compiler_params=pltpu.CompilerParams(vmem_limit_bytes=10 << 20),
            name="group_rows",
        )(chip.reshape(1), *members)
        length = jnp.broadcast_to(lengths, (8, LANES))
        far_count = sum(swap(length, bits) for bits in far_steps)
        places = jnp.stack(
            [place, vocab * home]
            + [(vocab ^ o) * shard_levels + place * width for o in range(vocab_size)]
        )

        early_plan, late_plan = plan[:late], plan[late:]

        def cost(work, arrays, extra):
            moved = sum(a.size * a.dtype.itemsize for a in arrays)
            flops = sum(2 * count_rows * span * size for _, _, size in work)
            return pl.CostEstimate(flops=flops, bytes_accessed=moved, transcendentals=extra)

        def limit(arrays, extra_mib):
            size = sum(a.size * a.dtype.itemsize for a in arrays) + 10 * count_rows * columns
            return pltpu.CompilerParams(vmem_limit_bytes=size + (extra_mib << 20))

        logits_shape = jax.ShapeDtypeStruct((count_rows, columns), jnp.float32)

        def pile_shape(work):
            held = len({p[0] for p in work})
            return jax.ShapeDtypeStruct((held, span, columns), head.dtype)

        early, early_pile = pl.pallas_call(
            functools.partial(early_kernel, early_plan),
            out_shape=(logits_shape, pile_shape(early_plan)),
            in_specs=[VMEM] * (1 + late),
            out_specs=(VMEM,) * 2,
            cost_estimate=cost(early_plan, [rows, *arrays[:late]], 0),
            compiler_params=limit([rows, *arrays[:late], *arrays[:late]], 2),
            name="early_logits",
        )(rows, *arrays[:late])
        logits, late_pile, stats = pl.pallas_call(
            functools.partial(stats_kernel, late_plan, width),
            out_shape=(
                logits_shape,
                pile_shape(late_plan),
                jax.ShapeDtypeStruct((8, count_rows), jnp.float32),
            ),
            in_specs=[SMEM] + [VMEM] * (4 + len(arrays) - late),
            out_specs=(VMEM,) * 3,
            cost_estimate=cost(late_plan, [rows, *arrays[late:]], count_rows * columns),
            compiler_params=limit([rows, *arrays[late:], *arrays[late:]], 2),
            name="row_stats",
        )(places, rows, facts, early, far_count, *arrays[late:])
        early_blocks, late_blocks = (sorted({p[0] for p in w}) for w in (early_plan, late_plan))
        where = {b: (0, i) for i, b in enumerate(early_blocks)}
        where |= {b: (1, i) for i, b in enumerate(late_blocks)}
        piles = [early_pile, late_pile]
        stats = jnp.concatenate([stats, swap(stats, CORE)])
        others = [swap(stats, SIDE), swap(stats, PAIR), swap(stats, SIDE | PAIR)]
        chunks = [range(0, blocks // 2), range(blocks // 2, blocks)]

        def sums_shape(chunk, members):
            shape = (len(chunk), members * home, span)
            return (
                jax.ShapeDtypeStruct(shape, jnp.bfloat16),
                jax.ShapeDtypeStruct(shape, jnp.float32),
            )

        work = [p for p in plan if p[0] in chunks[0]]
        send, keep, loss, grad = pl.pallas_call(
            functools.partial(grad_kernel, where, width, chunks[0]),
            out_shape=(
                *sums_shape(chunks[0], GROUP // 2),
                jax.ShapeDtypeStruct((8, LANES), jnp.float32),
                jax.ShapeDtypeStruct((count_rows, columns), jnp.bfloat16),
            ),
            in_specs=[SMEM] + [VMEM] * 9,
            out_specs=(VMEM,) * 4,
            cost_estimate=cost(work, piles, count_rows * columns),
            compiler_params=limit(piles, 8),
            name="grad_rows",
        )(places, count, facts, logits, stats, *others, *piles)
        send_rest, keep_rest = pl.pallas_call(
            functools.partial(rest_kernel, where, chunks[1]),
            out_shape=sums_shape(chunks[1], GROUP // 2),
            in_specs=[VMEM] * 3,
            out_specs=(VMEM,) * 2,
            cost_estimate=cost(work, piles, 0),
            compiler_params=limit(piles, 6),
            name="grad_rest",
        )(grad, *piles)

        def fold(taken, total, others, kept, sent):
            shape = (len(taken), len(kept) * home, span)
            return pl.pallas_call(
                functools.partial(fold_kernel, taken, kept, sent, home),
                out_shape=(
                    jax.ShapeDtypeStruct(shape, jnp.float32),
                    jax.ShapeDtypeStruct(shape, jnp.bfloat16),
                ),
                in_specs=[VMEM] * (1 + len(others)),
                out_specs=(VMEM,) * 2,
                compiler_params=pltpu.CompilerParams(vmem_limit_bytes=6 << 20),
            )(total, *others)

        sums, terms, pool = [None] * blocks, [None] * blocks, []
        routes = (
            (chunks[0], send, keep, (SIDE, (0, 2), (1, 3)), PAIR),
            (chunks[1], send_rest, keep_rest, (PAIR, (0, 1), (2, 3)), SIDE),
        )
        for chunk, out, total, (bits, kept, sent), last_bits in routes:
            arrived = swap(out, CORE)
            half = len(chunk) // 2
            steps = [list(chunk[:half]), list(chunk[half:])]
            firsts = []
            for step in steps:
                taken = [(chunk.index(b), 0, chunk.index(b)) for b in step]
                firsts.append(fold(taken, total, [arrived], kept, sent))
            incoming = [swap(f[1], bits) for f in firsts]
            for i, step in enumerate(steps):
                mine = [b ^ (bits >> 1) for b in step]
                held = [n for n, own in enumerate(steps) if mine[0] in own][0]
                mine.sort()
                taken = [
                    (steps[held].index(b), 0, step.index(b ^ (bits >> 1))) for b in mine
                ]
                keep_last, send_last = fold(taken, firsts[held][0], [incoming[i]], (0,), (1,))
                away = swap(send_last, last_bits)
                for n, b in enumerate(mine):
                    sums[b] = (len(pool), n)
                    terms[b ^ (last_bits >> 1)] = (len(pool) + 1, n)
                pool += [keep_last, away]

        shares = [
            swap(loss, far, bits) if far or bits else loss
            for far in range(0, dp_size, GROUP)
            for bits in range(vocab_size)
        ]
        final, loss = pl.pallas_call(
            functools.partial(final_kernel, sums, terms, len(shares)),
            out_shape=(
                jax.ShapeDtypeStruct((home, blocks * span), jnp.bfloat16),
                jax.ShapeDtypeStruct((1, 1), jnp.float32),
            ),
            in_specs=[SMEM] + [VMEM] * (len(pool) + len(shares)),
            out_specs=(VMEM, VMEM),
            scratch_shapes=[pltpu.VMEM((blocks, home, span), jnp.bfloat16)],
            compiler_params=pltpu.CompilerParams(vmem_limit_bytes=6 << 20),
            name="final_rows",
        )(chip.reshape(1), *pool, *shares)
        return final, loss.reshape(())

    return local


def solution(mesh):
    placed = (P(("dp", "vocab"), None), P(("dp", "vocab")), P("dp"), P("dp", "vocab"))
    sizes = mesh.shape["dp"], mesh.shape["vocab"]
    return jax.shard_map(
        build(*sizes),
        mesh=mesh,
        in_specs=placed,
        out_specs=(P(("dp", "vocab"), None), P()),
        check_vma=False,
    )
```

```python
import functools

import jax
import jax.numpy as jnp
from jax import lax
from jax.experimental import pallas as pl
from jax.experimental.pallas import tpu as pltpu
from jax.sharding import PartitionSpec as P


CORE, SIDE, PAIR, FAR = 1, 2, 4, 8
GROUP = FAR
LANES = 128
BASE = 128
VMEM = pl.BlockSpec(memory_space=pltpu.VMEM)
SMEM = pl.BlockSpec(memory_space=pltpu.SMEM)


def accumulate(plan, pieces, rows_ref, logits_ref, pile_ref):
    held = sorted({block for block, _, _ in plan})
    for (block, start, size), piece in zip(plan, pieces, strict=True):
        value = piece[...]
        pile_ref[held.index(block), :, start : start + size] = value
        logits_ref[:, start : start + size] += jnp.dot(
            rows_ref[block], value, preferred_element_type=jnp.float32
        )


def rows_kernel(blocks, chip_ref, *refs):
    *members, rows_ref, facts_ref, count_ref = refs
    home = members[0].shape[0]
    span = rows_ref.shape[2]
    lane = lax.broadcasted_iota(jnp.int32, (home, LANES), 1)
    total = None
    for r, member in enumerate(members):
        at = slice(r * home, (r + 1) * home)
        for block in range(blocks):
            rows_ref[block ^ chip_ref[0], at, :] = member[:, block * span : (block + 1) * span]
        notes = member[:, blocks * span :].astype(jnp.float32)
        target = (notes[:, 0:1] * BASE + notes[:, 1:2]).astype(jnp.int32)
        length = (notes[:, 2:3] * BASE + notes[:, 3:4]).astype(jnp.int32)
        facts_ref[at, :] = jnp.where(lane == LANES - 1, length, target)
        total = length[:1] if total is None else total + length[:1]
    count_ref[...] = jnp.broadcast_to(total, count_ref.shape)


def early_kernel(plan, rows_ref, *refs):
    *pieces, logits_ref, pile_ref = refs
    logits_ref[...] = jnp.zeros_like(logits_ref)
    accumulate(plan, pieces, rows_ref, logits_ref, pile_ref)


def middle_kernel(plan, rows_ref, early_ref, *refs):
    *pieces, logits_ref, pile_ref = refs
    logits_ref[...] = early_ref[...]
    accumulate(plan, pieces, rows_ref, logits_ref, pile_ref)


def stats_kernel(plan, width, place_ref, rows_ref, facts_ref, early_ref, far_ref, *refs):
    *pieces, logits_ref, pile_ref, stats_ref = refs
    count, total_width = logits_ref.shape
    logits_ref[...] = early_ref[...]
    accumulate(plan, pieces, rows_ref, logits_ref, pile_ref)
    target = facts_ref[:, :1]
    maxima = jnp.max(logits_ref[...], axis=1, keepdims=True)
    totals = jnp.zeros_like(maxima)
    hit_logit = jnp.zeros_like(maxima)
    lane = lax.broadcasted_iota(jnp.int32, (count, width), 1)
    for offset in range(total_width // width):
        tile = logits_ref[:, offset * width : (offset + 1) * width]
        totals += jnp.sum(jnp.exp(tile - maxima), axis=1, keepdims=True)
        hit = lane == target - place_ref[2 + offset]
        hit_logit += jnp.sum(jnp.where(hit, tile, 0.0), axis=1, keepdims=True)
    column = lax.broadcasted_iota(jnp.int32, (count, LANES), 1)
    packed = jnp.where(column == 0, maxima, jnp.where(column == 1, totals, hit_logit))
    packed = jnp.where(column == 3, far_ref[:1, :1].astype(jnp.float32), packed)
    stats_ref[...] = jnp.transpose(packed)[:8]


def by_place(values, place):
    for bit in (CORE, SIDE, PAIR):
        odd = lax.rem(place // bit, 2) == 1
        values = [jnp.where(odd, values[i ^ bit], values[i]) for i in range(GROUP)]
    return values


def tree_sum(values):
    while len(values) > 1:
        values = [a + b for a, b in zip(values[::2], values[1::2])]
    return values[0]


def grad_kernel(where, width, chunk, place_ref, count_ref, facts_ref, logits_ref, *refs):
    stats_refs, refs = refs[:4], refs[4:]
    *piles, send_ref, keep_ref, loss_ref, grad_ref = refs
    count, total_width = logits_ref.shape
    home = count // GROUP
    place = place_ref[0]
    members = []
    for k in range(GROUP):
        stats = stats_refs[k // 2][8 * (k % 2) : 8 * (k % 2) + 8, :]
        members.append(
            jnp.concatenate([stats[:, (r ^ k) * home : ((r ^ k) + 1) * home] for r in range(GROUP)], axis=1)
        )
    top = functools.reduce(jnp.maximum, [m[0:1] for m in members])
    terms = by_place([m[1:2] * jnp.exp(m[0:1] - top) for m in members], place)
    log_row = top + jnp.log(tree_sum(terms))
    hit_row = tree_sum(by_place([m[2:3] for m in members], place))
    columns = jnp.transpose(
        jnp.concatenate([log_row, hit_row, jnp.zeros((LANES - 2, count), jnp.float32)])
    )
    log_total, hit_logit = columns[:, 0:1], columns[:, 1:2]
    position = place_ref[1] + lax.rem(lax.broadcasted_iota(jnp.int32, (count, 1), 0), home)
    valid = (position < facts_ref[:, LANES - 1 :]).astype(jnp.float32)
    row_loss = valid * (log_total - hit_logit)
    sums = [
        jnp.sum(row_loss[r * home : (r + 1) * home], axis=0, keepdims=True) for r in range(GROUP)
    ]
    valid_count = count_ref[:1, :1].astype(jnp.float32) + sum(m[3:4, :1] for m in members)
    loss_ref[...] = jnp.broadcast_to(tree_sum(by_place(sums, place)) / valid_count, loss_ref.shape)
    weight = valid / valid_count
    target = facts_ref[:, :1]
    lane = lax.broadcasted_iota(jnp.int32, (count, width), 1)
    for offset in range(total_width // width):
        tile = slice(offset * width, (offset + 1) * width)
        hit = (lane == target - place_ref[2 + offset]).astype(jnp.float32)
        grad_ref[:, tile] = (weight * (jnp.exp(logits_ref[:, tile] - log_total) - hit)).astype(
            jnp.bfloat16
        )
    grad_product(where, chunk, piles, grad_ref, send_ref, keep_ref)


def grad_product(where, chunk, piles, grad_ref, send_ref, keep_ref):
    home = grad_ref.shape[0] // GROUP
    for row, block in enumerate(chunk):
        pile, index = where[block]
        total = lax.dot_general(
            grad_ref[...],
            piles[pile][index],
            (((1,), (1,)), ((), ())),
            preferred_element_type=jnp.float32,
        )
        for j in range(GROUP // 2):
            at = slice(j * home, (j + 1) * home)
            keep_ref[row, at] = total[2 * j * home : (2 * j + 1) * home]
            send_ref[row, at] = total[(2 * j + 1) * home : (2 * j + 2) * home].astype(jnp.bfloat16)


def rest_kernel(where, chunk, grad_ref, *refs):
    *piles, send_ref, keep_ref = refs
    grad_product(where, chunk, piles, grad_ref, send_ref, keep_ref)


def fold_kernel(taken, kept, sent, home, total_ref, *refs):
    *others, keep_ref, send_ref = refs
    for row, (block, array, index) in enumerate(taken):
        for j in range(len(kept)):
            at = slice(j * home, (j + 1) * home)
            rows = slice(kept[j] * home, (kept[j] + 1) * home)
            keep_ref[row, at] = total_ref[block, rows] + others[array][index, rows].astype(jnp.float32)
            rows = slice(sent[j] * home, (sent[j] + 1) * home)
            value = total_ref[block, rows] + others[array][index, rows].astype(jnp.float32)
            send_ref[row, at] = value.astype(jnp.bfloat16)


def final_kernel(sums, terms, shares, chip_ref, *refs):
    *arrays, out_ref, loss_ref, order_ref = refs
    loss_ref[...] = tree_sum([share[:1, :1] for share in arrays[len(arrays) - shares :]])
    blocks, _, span = order_ref.shape
    for block in range(blocks):
        (a, i), (b, j) = sums[block], terms[block]
        value = arrays[a][i] + arrays[b][j].astype(jnp.float32)
        order_ref[block ^ chip_ref[0]] = value.astype(jnp.bfloat16)
    for block in range(blocks):
        out_ref[:, block * span : (block + 1) * span] = order_ref[block]


def build(dp_size, vocab_size):
    assert dp_size >= 2 * GROUP and dp_size & (dp_size - 1) == 0
    assert vocab_size & (vocab_size - 1) == 0
    far_steps = range(GROUP, dp_size, GROUP)
    blocks = dp_size // 2

    def swap(value, dp_bits, vocab_bits=0):
        pairs = [
            (d * vocab_size + v, (d ^ dp_bits) * vocab_size + (v ^ vocab_bits))
            for d in range(dp_size)
            for v in range(vocab_size)
        ]
        return lax.ppermute(value, ("dp", "vocab"), pairs)

    def local(hidden, targets, lengths, head):
        dp = lax.axis_index("dp")
        vocab = lax.axis_index("vocab")
        core, chip, place = dp & 1, dp >> 1, dp & (GROUP - 1)
        home = hidden.shape[0]
        features = head.shape[0]
        shard_levels = head.shape[1]
        width = shard_levels // GROUP
        span = 2 * features
        arrays, plan = [], []

        def use(array, block, offset):
            plan.append((block, offset * width, width))
            arrays.append(array)

        def spread(block, piece):
            use(piece, block, 0)
            for bits in range(1, vocab_size):
                use(swap(piece, 0, bits), block, bits)

        def level_class(r):
            return lax.dynamic_slice_in_dim(head, (place ^ r) * width, width, 1)

        kinds = (0, PAIR, SIDE, SIDE | PAIR)
        arrived = swap(jnp.stack([level_class(CORE ^ r) for r in kinds]), CORE)
        ours = {}
        for i, r in enumerate(kinds):
            mine, other = level_class(r), arrived[i]
            ours[r] = jnp.where(
                core == 0, jnp.concatenate([mine, other]), jnp.concatenate([other, mine])
            )
        side = {0: swap(ours[SIDE], SIDE), PAIR: swap(ours[SIDE | PAIR], SIDE)}
        waves = [(ours, 0), (side, 1)]
        got = {}
        for source, bit in waves:
            got[bit] = source[0]
            got[(PAIR >> 1) | bit] = swap(source[PAIR], PAIR)
            for bits in far_steps:
                got[(bits >> 1) | bit] = swap(source[0], bits)
                got[((bits | PAIR) >> 1) | bit] = swap(source[PAIR], bits | PAIR)
        order = [0, 1, 2, *range(4, blocks, 4), *range(6, blocks, 4), 3, *range(5, blocks, 4), *range(7, blocks, 4)]
        cuts = [0, blocks // 2, 3 * blocks // 4, blocks]
        for block in order:
            spread(block, got[block])

        digits = [targets // BASE, targets % BASE, lengths // BASE, lengths % BASE]
        lane = jnp.arange(LANES)[None]
        notes = functools.reduce(
            lambda rest, i: jnp.where(lane == i, digits[i][:, None], rest), range(4), 0
        )
        mine = jnp.concatenate([hidden, notes.astype(hidden.dtype)], axis=1)
        pair = swap(mine, PAIR)
        beside = swap(mine, SIDE)
        both = swap(pair, SIDE)
        members = []
        for value in (mine, beside, pair, both):
            members += [value, swap(value, CORE)]
        count_rows, columns = GROUP * home, vocab_size * width
        rows, facts, count = pl.pallas_call(
            functools.partial(rows_kernel, blocks),
            out_shape=(
                jax.ShapeDtypeStruct((blocks, count_rows, span), hidden.dtype),
                jax.ShapeDtypeStruct((count_rows, LANES), jnp.int32),
                jax.ShapeDtypeStruct((8, LANES), jnp.int32),
            ),
            in_specs=[SMEM] + [VMEM] * GROUP,
            out_specs=(VMEM,) * 3,
            cost_estimate=pl.CostEstimate(
                flops=0, bytes_accessed=4 * count_rows * hidden.shape[1], transcendentals=0
            ),
            compiler_params=pltpu.CompilerParams(vmem_limit_bytes=10 << 20),
            name="group_rows",
        )(chip.reshape(1), *members)
        length = jnp.broadcast_to(lengths, (8, LANES))
        far_count = sum(swap(length, bits) for bits in far_steps)
        places = jnp.stack(
            [place, vocab * home]
            + [(vocab ^ o) * shard_levels + place * width for o in range(vocab_size)]
        )

        steps = [slice(i * vocab_size, j * vocab_size) for i, j in zip(cuts, cuts[1:])]
        early_plan, middle_plan, late_plan = (plan[step] for step in steps)
        early_arrays, middle_arrays, late_arrays = (arrays[step] for step in steps)

        def cost(work, arrays, extra):
            moved = sum(a.size * a.dtype.itemsize for a in arrays)
            flops = sum(2 * count_rows * span * size for _, _, size in work)
            return pl.CostEstimate(flops=flops, bytes_accessed=moved, transcendentals=extra)

        def limit(arrays, extra_mib):
            size = sum(a.size * a.dtype.itemsize for a in arrays) + 10 * count_rows * columns
            return pltpu.CompilerParams(vmem_limit_bytes=size + (extra_mib << 20))

        logits_shape = jax.ShapeDtypeStruct((count_rows, columns), jnp.float32)

        def pile_shape(work):
            held = len({p[0] for p in work})
            return jax.ShapeDtypeStruct((held, span, columns), head.dtype)

        logits, early_pile = pl.pallas_call(
            functools.partial(early_kernel, early_plan),
            out_shape=(logits_shape, pile_shape(early_plan)),
            in_specs=[VMEM] * (1 + len(early_arrays)),
            out_specs=(VMEM,) * 2,
            cost_estimate=cost(early_plan, [rows, *early_arrays], 0),
            compiler_params=limit([rows, *early_arrays, *early_arrays], 2),
            name="early_logits",
        )(rows, *early_arrays)
        logits, middle_pile = pl.pallas_call(
            functools.partial(middle_kernel, middle_plan),
            out_shape=(logits_shape, pile_shape(middle_plan)),
            in_specs=[VMEM] * (2 + len(middle_arrays)),
            out_specs=(VMEM,) * 2,
            cost_estimate=cost(middle_plan, [rows, *middle_arrays], 0),
            compiler_params=limit([rows, *middle_arrays, *middle_arrays], 4),
            name="middle_logits",
        )(rows, logits, *middle_arrays)
        logits, late_pile, stats = pl.pallas_call(
            functools.partial(stats_kernel, late_plan, width),
            out_shape=(
                logits_shape,
                pile_shape(late_plan),
                jax.ShapeDtypeStruct((8, count_rows), jnp.float32),
            ),
            in_specs=[SMEM] + [VMEM] * (4 + len(late_arrays)),
            out_specs=(VMEM,) * 3,
            cost_estimate=cost(late_plan, [rows, *late_arrays], count_rows * columns),
            compiler_params=limit([rows, *late_arrays, *late_arrays], 4),
            name="row_stats",
        )(places, rows, facts, logits, far_count, *late_arrays)
        where = {}
        for number, work in enumerate((early_plan, middle_plan, late_plan)):
            for index, block in enumerate(sorted({p[0] for p in work})):
                where[block] = number, index
        piles = [early_pile, middle_pile, late_pile]
        stats = jnp.concatenate([stats, swap(stats, CORE)])
        others = [swap(stats, SIDE), swap(stats, PAIR), swap(stats, SIDE | PAIR)]
        chunks = [range(0, blocks // 2), range(blocks // 2, blocks)]

        def sums_shape(chunk, members):
            shape = (len(chunk), members * home, span)
            return (
                jax.ShapeDtypeStruct(shape, jnp.bfloat16),
                jax.ShapeDtypeStruct(shape, jnp.float32),
            )

        work = [p for p in plan if p[0] in chunks[0]]
        send, keep, loss, grad = pl.pallas_call(
            functools.partial(grad_kernel, where, width, chunks[0]),
            out_shape=(
                *sums_shape(chunks[0], GROUP // 2),
                jax.ShapeDtypeStruct((8, LANES), jnp.float32),
                jax.ShapeDtypeStruct((count_rows, columns), jnp.bfloat16),
            ),
            in_specs=[SMEM] + [VMEM] * (7 + len(piles)),
            out_specs=(VMEM,) * 4,
            cost_estimate=cost(work, piles, count_rows * columns),
            compiler_params=limit(piles, 8),
            name="grad_rows",
        )(places, count, facts, logits, stats, *others, *piles)
        send_rest, keep_rest = pl.pallas_call(
            functools.partial(rest_kernel, where, chunks[1]),
            out_shape=sums_shape(chunks[1], GROUP // 2),
            in_specs=[VMEM] * (1 + len(piles)),
            out_specs=(VMEM,) * 2,
            cost_estimate=cost(work, piles, 0),
            compiler_params=limit(piles, 6),
            name="grad_rest",
        )(grad, *piles)

        def fold(taken, total, others, kept, sent):
            shape = (len(taken), len(kept) * home, span)
            return pl.pallas_call(
                functools.partial(fold_kernel, taken, kept, sent, home),
                out_shape=(
                    jax.ShapeDtypeStruct(shape, jnp.float32),
                    jax.ShapeDtypeStruct(shape, jnp.bfloat16),
                ),
                in_specs=[VMEM] * (1 + len(others)),
                out_specs=(VMEM,) * 2,
                compiler_params=pltpu.CompilerParams(vmem_limit_bytes=6 << 20),
            )(total, *others)

        sums, terms, pool = [None] * blocks, [None] * blocks, []
        routes = (
            (chunks[0], send, keep, (SIDE, (0, 2), (1, 3)), PAIR),
            (chunks[1], send_rest, keep_rest, (PAIR, (0, 1), (2, 3)), SIDE),
        )
        for chunk, out, total, (bits, kept, sent), last_bits in routes:
            arrived = swap(out, CORE)
            half = len(chunk) // 2
            steps = [list(chunk[:half]), list(chunk[half:])]
            firsts = []
            for step in steps:
                taken = [(chunk.index(b), 0, chunk.index(b)) for b in step]
                firsts.append(fold(taken, total, [arrived], kept, sent))
            incoming = [swap(f[1], bits) for f in firsts]
            for i, step in enumerate(steps):
                mine = [b ^ (bits >> 1) for b in step]
                held = [n for n, own in enumerate(steps) if mine[0] in own][0]
                mine.sort()
                taken = [
                    (steps[held].index(b), 0, step.index(b ^ (bits >> 1))) for b in mine
                ]
                keep_last, send_last = fold(taken, firsts[held][0], [incoming[i]], (0,), (1,))
                away = swap(send_last, last_bits)
                for n, b in enumerate(mine):
                    sums[b] = (len(pool), n)
                    terms[b ^ (last_bits >> 1)] = (len(pool) + 1, n)
                pool += [keep_last, away]

        shares = [
            swap(loss, far, bits) if far or bits else loss
            for far in range(0, dp_size, GROUP)
            for bits in range(vocab_size)
        ]
        final, loss = pl.pallas_call(
            functools.partial(final_kernel, sums, terms, len(shares)),
            out_shape=(
                jax.ShapeDtypeStruct((home, blocks * span), jnp.bfloat16),
                jax.ShapeDtypeStruct((1, 1), jnp.float32),
            ),
            in_specs=[SMEM] + [VMEM] * (len(pool) + len(shares)),
            out_specs=(VMEM, VMEM),
            scratch_shapes=[pltpu.VMEM((blocks, home, span), jnp.bfloat16)],
            compiler_params=pltpu.CompilerParams(vmem_limit_bytes=6 << 20),
            name="final_rows",
        )(chip.reshape(1), *pool, *shares)
        return final, loss.reshape(())

    return local


def solution(mesh):
    placed = (P(("dp", "vocab"), None), P(("dp", "vocab")), P("dp"), P("dp", "vocab"))
    sizes = mesh.shape["dp"], mesh.shape["vocab"]
    return jax.shard_map(
        build(*sizes),
        mesh=mesh,
        in_specs=placed,
        out_specs=(P(("dp", "vocab"), None), P()),
        check_vma=False,
    )
```
